256 devices in a mesh: seq: 64 (over z, y, core), head: 4 (over x).
Axes of the slice: x: 4, y: 4, z: 8, core: 2. Of those that a mesh axis runs over, the one named last changes fastest.
Arguments:
- hidden_in: bfloat16 [16384, 2048], P('seq', 'head'), may hold values from -6 to 6
- ple_in: bfloat16 [16384, 256], P('seq'), may hold values from -6 to 6
- group_map: int32 [128, 1], replicated, may hold values from 0 to 11
- prompt_len: int32 [12], replicated, may hold values from 1 to 8192, as said below
- cache: bfloat16 [12, 8192, 1024], P(None, 'seq', 'head'), may hold values from -6 to 6
- w_query: bfloat16 [2048, 2048], P(None, 'head'), may hold values from -0.125 to 0.125
- key_value_weight: bfloat16 [2048, 1024], P(None, 'head'), may hold values from -0.125 to 0.125
- w_out: bfloat16 [2048, 2048], P('head'), may hold values from -0.125 to 0.125
- in_gain: float32 [2048], replicated, may hold values from 0.5 to 2
- q_gain: float32 [256], replicated
- k_gain: float32 [256], replicated, may hold values from 0.5 to 2
- post_gain: float32 [2048], replicated, may hold values from 0.5 to 2
- laurel_left: bfloat16 [2048, 64], replicated, may hold values from -0.125 to 0.125
- laurel_right: bfloat16 [64, 2048], replicated, may hold values from -0.75 to 0.75
- laurel_gain: float32 [2048], replicated, may hold values from 0.5 to 2
- w_plgate: bfloat16 [2048, 256], replicated, may hold values from -0.125 to 0.125
- w_plproj: bfloat16 [256, 2048], replicated, may hold values from -0.375 to 0.375
- ple_gain: float32 [2048], replicated, may hold values from 0.5 to 2
Outputs:
- layer_out: bfloat16 [16384, 2048], P('seq', 'head')
The draws below stay inside these ranges and needn't reach their ends.
Inputs may be any that keep to these rules, and one draw needn't show every extreme that they name: `group_map`: every one of the 12 groups is named by at least one request. `prompt_len`: some group's prompt fills all 8192 slots.
All inputs are finite; a program needn't handle non-finite values.
Results may differ from the reference program's by a relative error of at most 0.011.
The reference program's roundings to bfloat16 on the way count: a program that leaves them out, or rounds other values in their place, can miss the bound.
Values may be sent and summed in bfloat16 or wider, within the bound.
A program may use at most 128 MiB of HBM per device.

```python
import math
import jax
import jax.numpy as jnp
from jax import lax

MODEL_WIDTH = 2048
QUERY_HEADS = 8
KEY_VALUE_HEADS = 2
HEAD_SIZE = 256
R = 64
PLD = 256
NEW = 128
PROMPT_SLOTS = 8192
PROMPT_GROUPS = 12
REQUESTS = 128
TOKEN_TOTAL = 16384


def draw_prompt_len(key, part):
    first_key, second_key = jax.random.split(key)
    lengths = jax.random.randint(first_key, (PROMPT_GROUPS,), 1, PROMPT_SLOTS + 1)
    chosen = jax.random.randint(second_key, (), 0, PROMPT_GROUPS)
    return jnp.where(jnp.arange(PROMPT_GROUPS) == chosen, PROMPT_SLOTS, lengths).astype(jnp.int32)


def draw_q_gain(key, part):
    values = jnp.exp(jax.random.uniform(key, (HEAD_SIZE,), jnp.float32, -0.69, 0.69)) * 0.0625
    return values.astype(jnp.float32)


def block_scale(own_key, shape, shards, smallest, top_value):
    loudness, own = 1.0, jax.random.fold_in(own_key, 6)
    for axis_at, parts in shards:
        heights = jnp.exp(jax.random.uniform(jax.random.fold_in(own, axis_at), (parts,), jnp.float32, smallest / len(shards), top_value / len(shards)))
        loudness = loudness * jnp.repeat(heights, shape[axis_at] // parts).reshape([-1 if axis == axis_at else 1 for axis in range(len(shape))])
    return loudness


def distinct(stream_key, rows, number_of, top, lift):
    order = jax.random.permutation(jax.random.fold_in(stream_key, 1), number_of)
    favour = order
    for power in range(3):
        favour = favour * favour // number_of
    favour = favour * lift // number_of
    tickets = jax.random.randint(jax.random.fold_in(stream_key, 2), (rows, number_of), 0, 4096) + favour
    holders = jax.random.permutation(jax.random.fold_in(stream_key, 3), rows)[jnp.arange(number_of) % rows]
    tickets = jnp.where(jnp.arange(rows)[:, None] == holders[None, :], 1 << 14, tickets)
    score = tickets * number_of + jnp.arange(number_of)
    return lax.top_k(score.astype(jnp.int32), top)[1].astype(jnp.int32)


def scatter_about(own_key, extent, deviation, reach, cuts=(), kind=jnp.bfloat16):
    result = jax.random.normal(own_key, extent, jnp.float32) * deviation
    if len(cuts) > 0:
        result = block_scale(own_key, extent, cuts, -0.22, 0.18) * result
    return jnp.clip(result, min=-reach, max=reach).astype(kind)


def setup_inputs(seed: int = 0) -> dict:
    arg_keys = jax.random.split(jax.random.key(seed), 19)
    hidden_in = scatter_about(arg_keys[0], (TOKEN_TOTAL, MODEL_WIDTH), 1.0, 6.0, ((0, 64), (1, 4)))
    ple_in = scatter_about(arg_keys[1], (TOKEN_TOTAL, PLD), 1.0, 6.0, ((0, 64),))
    group_map = distinct(arg_keys[2], REQUESTS, PROMPT_GROUPS, 1, 1365)
    prompt_len = draw_prompt_len(jax.random.fold_in(arg_keys[18], 71), 0)
    cache = scatter_about(arg_keys[4], (PROMPT_GROUPS, PROMPT_SLOTS, 2 * KEY_VALUE_HEADS * HEAD_SIZE), 1.0, 6.0, ((1, 64), (2, 4)))
    w_query = scatter_about(arg_keys[5], (MODEL_WIDTH, QUERY_HEADS * HEAD_SIZE), MODEL_WIDTH ** -0.5, 0.125, ((1, 4),))
    key_value_weight = scatter_about(arg_keys[6], (MODEL_WIDTH, 2 * KEY_VALUE_HEADS * HEAD_SIZE), MODEL_WIDTH ** -0.5, 0.125, ((1, 4),))
    w_out = scatter_about(arg_keys[7], (QUERY_HEADS * HEAD_SIZE, MODEL_WIDTH), (QUERY_HEADS * HEAD_SIZE) ** -0.5, 0.125, ((0, 4),))
    in_gain = jnp.clip(jnp.exp(jax.random.uniform(arg_keys[8], (MODEL_WIDTH,), jnp.float32, math.log(0.5), math.log(2.0))), 0.5, 2.0)
    q_gain = draw_q_gain(jax.random.fold_in(arg_keys[18], 71), 0)
    k_gain = jnp.clip(jnp.exp(jax.random.uniform(arg_keys[10], (HEAD_SIZE,), jnp.float32, math.log(0.5), math.log(2.0))), 0.5, 2.0)
    post_gain = jnp.clip(jnp.exp(jax.random.uniform(arg_keys[11], (MODEL_WIDTH,), jnp.float32, math.log(0.5), math.log(2.0))), 0.5, 2.0)
    laurel_left = scatter_about(arg_keys[12], (MODEL_WIDTH, R), MODEL_WIDTH ** -0.5, 0.125)
    laurel_right = scatter_about(arg_keys[13], (R, MODEL_WIDTH), R ** -0.5, 0.75)
    laurel_gain = jnp.clip(jnp.exp(jax.random.uniform(arg_keys[14], (MODEL_WIDTH,), jnp.float32, math.log(0.5), math.log(2.0))), 0.5, 2.0)
    w_plgate = scatter_about(arg_keys[15], (MODEL_WIDTH, PLD), MODEL_WIDTH ** -0.5, 0.125)
    w_plproj = scatter_about(arg_keys[16], (PLD, MODEL_WIDTH), PLD ** -0.5, 0.375)
    ple_gain = jnp.clip(jnp.exp(jax.random.uniform(arg_keys[17], (MODEL_WIDTH,), jnp.float32, math.log(0.5), math.log(2.0))), 0.5, 2.0)
    return {"hidden_in": hidden_in, "ple_in": ple_in, "group_map": group_map, "prompt_len": prompt_len, "cache": cache, "w_query": w_query, "key_value_weight": key_value_weight, "w_out": w_out, "in_gain": in_gain, "q_gain": q_gain, "k_gain": k_gain, "post_gain": post_gain, "laurel_left": laurel_left, "laurel_right": laurel_right, "laurel_gain": laurel_gain, "w_plgate": w_plgate, "w_plproj": w_plproj, "ple_gain": ple_gain}


epsilon = 1e-06
theta_base = 1000000.0

def norm_rows(values):
    return values * lax.rsqrt(lax.optimization_barrier(jnp.mean(values * values, axis=-1, keepdims=True)) + epsilon)

def rotate(values, positions):
    half_width = values.shape[-1] // 2
    inverse = theta_base ** (-jnp.arange(half_width, dtype=jnp.float32) / half_width)
    angles = positions.astype(jnp.float32)[:, None] * inverse[None, :]
    cosine = jnp.cos(angles)[:, None, :]
    sine_part = jnp.sin(angles)[:, None, :]
    front_half = values[..., :half_width]
    back_half = values[..., half_width:]
    return jnp.concatenate([front_half * cosine - back_half * sine_part, back_half * cosine + front_half * sine_part], axis=-1)

def contract_last(left_rows, right_rows):
    return lax.dot_general(left_rows, right_rows, (((1,), (1,)), ((), ())), preferred_element_type=jnp.float32)

def attend(queries, cached_keys, cached_values, new_keys, new_values, length):
    tokens, head_count, head_width = queries.shape
    query_rows = queries.reshape(tokens * head_count, head_width)
    cache_scores = contract_last(query_rows, cached_keys)
    fresh_scores = contract_last(query_rows, new_keys)
    valid_keys = jnp.arange(cached_keys.shape[0], dtype=jnp.int32) < length
    row_token = jnp.arange(tokens * head_count, dtype=jnp.int32) // head_count
    causal = jnp.arange(tokens, dtype=jnp.int32)[None, :] <= row_token[:, None]
    cache_scores = jnp.where(valid_keys[None, :], cache_scores, -1e+30)
    fresh_scores = jnp.where(causal, fresh_scores, -1e+30)
    highest = jnp.maximum(lax.optimization_barrier(jnp.max(cache_scores, axis=1)), lax.optimization_barrier(jnp.max(fresh_scores, axis=1)))
    cache_weights = jnp.exp(cache_scores - highest[:, None])
    fresh_weights = jnp.exp(fresh_scores - highest[:, None])
    totals = lax.optimization_barrier(jnp.sum(cache_weights, axis=1)) + lax.optimization_barrier(jnp.sum(fresh_weights, axis=1))
    mixture = jnp.dot(cache_weights.astype(jnp.bfloat16), cached_values, preferred_element_type=jnp.float32)
    mixture = mixture + jnp.dot(fresh_weights.astype(jnp.bfloat16), new_values, preferred_element_type=jnp.float32)
    return (mixture / totals[:, None]).reshape(tokens, head_count, head_width).astype(jnp.bfloat16)

def finish(residual, normed_input, projected, ple_in, post_gain, laurel_left, laurel_right, laurel_gain, w_plgate, w_plproj, ple_gain):
    attn_branch = norm_rows(projected) * post_gain
    low_rank = jnp.dot(normed_input, laurel_left, preferred_element_type=jnp.float32).astype(jnp.bfloat16)
    laurel_out = jnp.dot(low_rank, laurel_right, preferred_element_type=jnp.float32)
    laurel_branch = normed_input.astype(jnp.float32) + norm_rows(laurel_out) * laurel_gain
    combined = (residual + attn_branch + laurel_branch) * math.sqrt(0.5)
    gate_in = jnp.dot(combined.astype(jnp.bfloat16), w_plgate, preferred_element_type=jnp.float32)
    gated = (jax.nn.gelu(gate_in, approximate=True) * ple_in.astype(jnp.float32)).astype(jnp.bfloat16)
    ple_out = jnp.dot(gated, w_plproj, preferred_element_type=jnp.float32)
    return (combined + norm_rows(ple_out) * ple_gain).astype(jnp.bfloat16)

def reference(hidden_in, ple_in, group_map, prompt_len, cache, w_query, key_value_weight, w_out, in_gain, q_gain, k_gain, post_gain, laurel_left, laurel_right, laurel_gain, w_plgate, w_plproj, ple_gain):
    residual = hidden_in.astype(jnp.float32)
    normed_input = (norm_rows(residual) * in_gain).astype(jnp.bfloat16)
    group_list = group_map[:, 0]
    lengths = prompt_len[group_list]
    positions = (lengths[:, None] + jnp.arange(NEW, dtype=jnp.int32)[None, :]).reshape(-1)
    queries = jnp.dot(normed_input, w_query, preferred_element_type=jnp.float32).reshape(TOKEN_TOTAL, QUERY_HEADS, HEAD_SIZE)
    queries = rotate(norm_rows(queries) * q_gain, positions).astype(jnp.bfloat16)
    fresh_projected = jnp.dot(normed_input, key_value_weight, preferred_element_type=jnp.float32).reshape(TOKEN_TOTAL, KEY_VALUE_HEADS, 2, HEAD_SIZE)
    new_keys = rotate(norm_rows(fresh_projected[:, :, 0]) * k_gain, positions).astype(jnp.bfloat16)
    new_values = norm_rows(fresh_projected[:, :, 1]).astype(jnp.bfloat16)
    group_requests = QUERY_HEADS // KEY_VALUE_HEADS

    def one_request(request_item):
        start = request_item * NEW
        layer_block = lax.dynamic_index_in_dim(cache, group_list[request_item], 0, keepdims=False).reshape(PROMPT_SLOTS, KEY_VALUE_HEADS, 2, HEAD_SIZE)
        query_part = lax.dynamic_slice_in_dim(queries, start, NEW)
        key_part = lax.dynamic_slice_in_dim(new_keys, start, NEW)
        value_part = lax.dynamic_slice_in_dim(new_values, start, NEW)
        pieces = []
        for key_value_head in range(KEY_VALUE_HEADS):
            pieces.append(attend(query_part[:, key_value_head * group_requests:(key_value_head + 1) * group_requests], layer_block[:, key_value_head, 0], layer_block[:, key_value_head, 1], key_part[:, key_value_head], value_part[:, key_value_head], lengths[request_item]))
        return jnp.concatenate(pieces, axis=1)
    attended = lax.map(one_request, jnp.arange(REQUESTS, dtype=jnp.int32)).reshape(TOKEN_TOTAL, QUERY_HEADS * HEAD_SIZE)
    projected = jnp.dot(attended, w_out, preferred_element_type=jnp.float32)
    return finish(residual, normed_input, projected, ple_in, post_gain, laurel_left, laurel_right, laurel_gain, w_plgate, w_plproj, ple_gain)
```

```python
import functools
import math

import jax
import jax.numpy as jnp
import numpy as np
from jax import lax
from jax.experimental import pallas as pl
from jax.experimental.pallas import tpu as pltpu
from jax.sharding import PartitionSpec as P

MESH = pl.DeviceIdType.MESH
BF16 = jnp.bfloat16
F32 = jnp.float32

NEW = 128
NZ, NY, NC, NX = 8, 4, 2, 4
GROUPS = 12
BLOCK = 128
WIDTH = 2048
SHARE = WIDTH // NX
HEAD = 256
HALF = HEAD // 2
ROWS = 2 * NEW
OWN = ROWS // NX
SPAN = NY * NC * BLOCK
EPSILON = 1e-06
THETA = 1000000.0
LOW = -1e30


def place():
    s = lax.axis_index("seq")
    x = lax.axis_index("head")
    c = lax.rem(s, NC)
    y = lax.rem(lax.div(s, NC), NY)
    z = lax.div(s, NC * NY)
    return s, x, z, y, c


def seq_of(z, y, c):
    return (z * NY + y) * NC + c


def norm_rows(values):
    return values * lax.rsqrt(jnp.mean(values * values, axis=-1, keepdims=True) + EPSILON)


def greet(devices):
    barrier = pltpu.get_barrier_semaphore()
    for device in devices:
        pl.semaphore_signal(barrier, inc=1, device_id=device, device_id_type=MESH)
    pl.semaphore_wait(barrier, len(devices))


def send(src, dst, send_sem, recv_sem, device):
    copy = pltpu.make_async_remote_copy(
        src_ref=src,
        dst_ref=dst,
        send_sem=send_sem,
        recv_sem=recv_sem,
        device_id=device,
        device_id_type=MESH,
    )
    copy.start()
    return copy


def gather_kernel(
    groups_ref,
    lens_ref,
    inverse_ref,
    in_gain_ref,
    q_gain_ref,
    k_gain_ref,
    left_ref,
    right_ref,
    laurel_gain_ref,
    hidden_ref,
    cache_ref,
    wq_ref,
    wkv_ref,
    kv_ref,
    q_ref,
    fresh_ref,
    base_ref,
    meta_ref,
    hid,
    normed,
    wq,
    wkv,
    own_cache,
    own_q,
    own_fresh,
    local_sem,
    h_send,
    h_recv,
    c_send,
    c_recv,
    b_send,
    b_recv,
    q_send,
    q_recv,
    f_send,
    f_recv,
):
    s, x, z, y, c = place()
    part = lax.rem(x, 2)
    other = 1 - part
    up_y, down_y = lax.rem(y + 1, NY), lax.rem(y + NY - 1, NY)
    far_y = lax.rem(y + 2, NY)
    up_z, down_z = lax.rem(z + 1, NZ), lax.rem(z + NZ - 1, NZ)
    x_mate = x + 1 - 2 * part
    dev_yu, dev_yd = (seq_of(z, up_y, c), x), (seq_of(z, down_y, c), x)
    dev_zu, dev_zd = (seq_of(up_z, y, c), x), (seq_of(down_z, y, c), x)
    dev_mate = (s, x_mate)
    dev_core = (seq_of(z, y, 1 - c), x)
    x_peers = [(s, lax.rem(x + step, NX)) for step in range(1, NX)]

    take_hidden = pltpu.make_async_copy(hidden_ref, hid.at[x], local_sem.at[0])
    take_wq = pltpu.make_async_copy(wq_ref, wq, local_sem.at[1])
    take_wkv = pltpu.make_async_copy(wkv_ref, wkv, local_sem.at[2])
    take_cache = pltpu.make_async_copy(cache_ref, own_cache, local_sem.at[3])
    for copy in (take_hidden, take_wq, take_wkv, take_cache):
        copy.start()

    greet(x_peers + [dev_yu, dev_yd, dev_zu, dev_zd, dev_core])

    hidden_copies = [
        send(hidden_ref, hid.at[x], h_send.at[step], h_recv.at[step], x_peers[step])
        for step in range(NX - 1)
    ]
    mine = kv_ref.at[part, y, c]
    cache_up = send(cache_ref, mine, c_send.at[0], c_recv.at[0], dev_yu)
    cache_down = send(cache_ref, mine, c_send.at[1], c_recv.at[1], dev_yd)
    cache_x = send(cache_ref, mine, c_send.at[2], c_recv.at[2], dev_mate)

    def to_core(index, which, row):
        ref = kv_ref.at[which, row, c]
        src = cache_ref if index == 0 else ref
        return send(src, ref, b_send.at[index], b_recv.at[index], dev_core)

    core_copies = [to_core(0, part, y)]
    take_cache.wait()
    put_cache = pltpu.make_async_copy(own_cache, mine, local_sem.at[3])
    put_cache.start()

    row = lax.broadcasted_iota(jnp.int32, (ROWS, HALF), 0)
    lens = [lens_ref[groups_ref[2 * s + r, 0]] for r in range(2)]
    first = jnp.where(row < NEW, lens[0], lens[1] - NEW)
    angles = (first + row).astype(F32) * inverse_ref[...]
    cosine, sine = jnp.cos(angles), jnp.sin(angles)
    for far in range(NZ):
        for r in range(2):
            group = groups_ref[2 * seq_of(far, y, c) + r, 0]
            meta_ref[0, 2 * far + r] = group
            meta_ref[1, 2 * far + r] = lens_ref[group]

    def rotate(values):
        front, back = values[:, :HALF], values[:, HALF:]
        return jnp.concatenate(
            [front * cosine - back * sine, back * cosine + front * sine], axis=1
        )

    take_hidden.wait()
    for copy in hidden_copies:
        copy.wait_recv()
    total = jnp.zeros((ROWS, 1), F32)
    for k in range(NX):
        block = hid[k].astype(F32)
        total = total + jnp.sum(block * block, axis=1, keepdims=True)
    scale = lax.rsqrt(total / WIDTH + EPSILON)
    for k in range(NX):
        gain = in_gain_ref[:, k * SHARE : (k + 1) * SHARE]
        normed[k] = (hid[k].astype(F32) * scale * gain).astype(BF16)
    take_wq.wait()
    for head in range(2):
        value = jnp.zeros((ROWS, HEAD), F32)
        for k in range(NX):
            value = value + jnp.dot(
                normed[k],
                wq[k * SHARE : (k + 1) * SHARE, head * HEAD : (head + 1) * HEAD],
                preferred_element_type=F32,
            )
        value = rotate(norm_rows(value) * q_gain_ref[...]).astype(BF16)
        for r in range(2):
            own_q[r, head] = value[r * NEW : (r + 1) * NEW]
    take_wkv.wait()
    value = jnp.zeros((ROWS, HEAD), F32)
    for k in range(NX):
        value = value + jnp.dot(
            normed[k], wkv[k * SHARE : (k + 1) * SHARE, :], preferred_element_type=F32
        )
    value = norm_rows(value)
    own_fresh[...] = jnp.where(part == 0, rotate(value * k_gain_ref[...]), value).astype(BF16)

    put_q = pltpu.make_async_copy(own_q, q_ref.at[z], local_sem.at[0])
    put_q.start()

    ups, downs = {}, {}

    def q_up(step, piece):
        origin = lax.rem(z + NZ - step, NZ)
        ref = q_ref.at[origin, piece]
        src = own_q.at[piece] if step == 0 else ref
        ups[step, piece] = send(
            src, ref, q_send.at[0, step, piece], q_recv.at[0, step, piece], dev_zu
        )

    def q_down(step, piece):
        origin = lax.rem(z + step, NZ)
        ref = q_ref.at[origin, piece]
        src = own_q.at[piece] if step == 0 else ref
        downs[step, piece] = send(
            src, ref, q_send.at[1, step, piece], q_recv.at[1, step, piece], dev_zd
        )

    q_up(0, 0)
    q_down(0, 1)
    q_up(0, 1)
    q_down(0, 0)
    fresh_copy = send(own_fresh, fresh_ref.at[part], f_send, f_recv, dev_mate)
    put_fresh = pltpu.make_async_copy(own_fresh, fresh_ref.at[part], local_sem.at[1])
    put_fresh.start()

    def q_pass(step):
        ups[step - 1, 0].wait_recv()
        q_up(step, 0)
        downs[step - 1, 1].wait_recv()
        q_down(step, 1)
        ups[step - 1, 1].wait_recv()
        if step < 3:
            q_up(step, 1)
        downs[step - 1, 0].wait_recv()
        if step < 3:
            q_down(step, 0)

    half = GROUPS // 2
    cache_up.wait_recv()
    low = kv_ref.at[part, down_y, c, pl.ds(0, half)]
    far_up = send(low, low, c_send.at[3], c_recv.at[3], dev_yu)
    core_copies.append(to_core(1, part, down_y))
    cache_down.wait_recv()
    high = kv_ref.at[part, up_y, c, pl.ds(half, half)]
    far_down = send(high, high, c_send.at[4], c_recv.at[4], dev_yd)
    core_copies.append(to_core(2, part, up_y))
    cache_x.wait_recv()
    second = kv_ref.at[other, y, c]
    other_up = send(second, second, c_send.at[5], c_recv.at[5], dev_yu)
    other_down = send(second, second, c_send.at[6], c_recv.at[6], dev_yd)
    core_copies.append(to_core(3, other, y))
    q_pass(1)
    far_up.wait_recv()
    far_down.wait_recv()
    distant = kv_ref.at[part, far_y, c]
    far_x = send(distant, distant, c_send.at[7], c_recv.at[7], dev_mate)
    core_copies.append(to_core(4, part, far_y))
    q_pass(2)

    own_rows = pl.ds(pl.multiple_of(x * OWN, OWN), OWN)
    low_rank = jnp.zeros((OWN, left_ref.shape[1]), F32)
    for k in range(NX):
        low_rank = low_rank + jnp.dot(
            normed[k, own_rows, :],
            left_ref[k * SHARE : (k + 1) * SHARE, :],
            preferred_element_type=F32,
        )
    laurel = jnp.dot(low_rank.astype(BF16), right_ref[...], preferred_element_type=F32)
    laurel = norm_rows(laurel) * laurel_gain_ref[...]
    for k in range(NX):
        cols = slice(k * SHARE, (k + 1) * SHARE)
        base_ref[:, cols] = (
            hid[k, own_rows, :].astype(F32)
            + normed[k, own_rows, :].astype(F32)
            + laurel[:, cols]
        )

    q_pass(3)
    other_up.wait_recv()
    core_copies.append(to_core(5, other, down_y))
    other_down.wait_recv()
    core_copies.append(to_core(6, other, up_y))
    far_x.wait_recv()
    core_copies.append(to_core(7, other, far_y))
    ups[3, 0].wait_recv()
    downs[3, 1].wait_recv()
    fresh_copy.wait_recv()
    for copy in core_copies:
        copy.wait_recv()
    put_cache.wait()
    put_q.wait()
    put_fresh.wait()
    for copy in hidden_copies + core_copies + [
        cache_up,
        cache_down,
        cache_x,
        far_up,
        far_down,
        other_up,
        other_down,
        far_x,
        fresh_copy,
    ]:
        copy.wait_send()
    for copy in list(ups.values()) + list(downs.values()):
        copy.wait_send()


def attend_kernel(meta_ref, q_ref, k_ref, v_ref, fresh_ref, out_ref, lse_ref, m_sc, l_sc, acc):
    i = pl.program_id(0)
    s, x, z, y, c = place()
    live = meta_ref[1, i] - z * SPAN
    rows = q_ref[...].reshape(ROWS, HEAD)

    @pl.when(live <= 0)
    def _():
        m_sc[...] = jnp.full_like(m_sc, LOW)
        l_sc[...] = jnp.zeros_like(l_sc)
        acc[...] = jnp.zeros_like(acc)

    @pl.when(live > 0)
    def _():
        keys = k_ref[...].reshape(SPAN, HEAD)
        values = v_ref[...].reshape(SPAN, HEAD)
        scores = lax.dot_general(
            rows, keys, (((1,), (1,)), ((), ())), preferred_element_type=F32
        )
        slot = lax.broadcasted_iota(jnp.int32, (1, SPAN), 1)
        scores = jnp.where(slot < live, scores, LOW)
        top = jnp.max(scores, axis=1, keepdims=True)
        weights = jnp.exp(scores - top)
        m_sc[...] = jnp.broadcast_to(top, m_sc.shape)
        l_sc[...] = jnp.broadcast_to(jnp.sum(weights, axis=1, keepdims=True), l_sc.shape)
        acc[...] = jnp.dot(weights.astype(BF16), values, preferred_element_type=F32)

    @pl.when(lax.div(i, 2) == z)
    def _():
        mine = pl.ds(pl.multiple_of(lax.rem(i, 2) * NEW, NEW), NEW)
        scores = lax.dot_general(
            rows, fresh_ref[0, mine, :], (((1,), (1,)), ((), ())), preferred_element_type=F32
        )
        token = lax.rem(lax.broadcasted_iota(jnp.int32, (ROWS, NEW), 0), NEW)
        slot = lax.broadcasted_iota(jnp.int32, (ROWS, NEW), 1)
        scores = jnp.where(slot <= token, scores, LOW)
        before = m_sc[:, :1]
        top = jnp.maximum(before, jnp.max(scores, axis=1, keepdims=True))
        weights = jnp.exp(scores - top)
        keep = jnp.exp(before - top)
        m_sc[...] = jnp.broadcast_to(top, m_sc.shape)
        l_sc[...] = l_sc[...] * keep + jnp.sum(weights, axis=1, keepdims=True)
        acc[...] = acc[...] * keep + jnp.dot(
            weights.astype(BF16), fresh_ref[1, mine, :], preferred_element_type=F32
        )

    some = l_sc[...] > 0
    amount = jnp.where(some, l_sc[...], 1.0)
    out_ref[0] = (acc[...] / amount[:, :1]).astype(BF16)
    lse = jnp.where(some, m_sc[...] + jnp.log(amount), LOW)
    lse_ref[0] = jnp.transpose(lse)[:8]


def merge(first, second):
    rows_a, lse_a = first
    rows_b, lse_b = second
    top = jnp.maximum(lse_a, lse_b)
    wa, wb = jnp.exp(lse_a - top), jnp.exp(lse_b - top)
    total = wa + wb
    return rows_a * (wa / total) + rows_b * (wb / total), top + jnp.log(total)


def finish_kernel(
    part_ref,
    lse_ref,
    base_ref,
    ple_ref,
    post_gain_ref,
    ple_gain_ref,
    wout_ref,
    wgate_ref,
    wproj_ref,
    out_ref,
    part,
    wout,
    wgate,
    wproj,
    o_out,
    l_out,
    o_in,
    l_in,
    p_out,
    p_in,
    res,
    local_sem,
    o_send,
    o_recv,
    l_send,
    l_recv,
    p_send,
    p_recv,
    r_send,
    r_recv,
):
    s, x, z, y, c = place()
    up_z, down_z = lax.rem(z + 1, NZ), lax.rem(z + NZ - 1, NZ)
    dev_zu, dev_zd = (seq_of(up_z, y, c), x), (seq_of(down_z, y, c), x)
    x_peers = [(s, lax.rem(x + step, NX)) for step in range(1, NX)]

    take_part = pltpu.make_async_copy(part_ref, part, local_sem.at[0])
    take_wout = pltpu.make_async_copy(wout_ref, wout, local_sem.at[1])
    take_wgate = pltpu.make_async_copy(wgate_ref, wgate, local_sem.at[2])
    take_wproj = pltpu.make_async_copy(wproj_ref, wproj, local_sem.at[3])
    for copy in (take_part, take_wout, take_wgate, take_wproj):
        copy.start()
    greet(x_peers + [dev_zu, dev_zd])
    take_part.wait()

    def column(block):
        return jnp.transpose(block)[:, :1]

    copies = {}
    reach = {(0, 0): 4, (0, 1): 3, (1, 0): 3, (1, 1): 4}

    def target(way, r, step):
        distance = reach[way, r] - step
        return lax.rem(z + distance, NZ) if way == 0 else lax.rem(z + NZ - distance, NZ)

    def mine(index):
        return part[index].astype(F32), column(lse_ref[index])

    def arrived(way, r, step):
        o_copy, l_copy = copies[way, r, step]
        o_copy.wait_recv()
        l_copy.wait_recv()
        return o_in[way, r, step].astype(F32), column(l_in[way, r, step])

    def hop(way, r, step):
        index = 2 * target(way, r, step) + r
        if step == 0:
            o_src, l_src = part.at[index], lse_ref.at[index]
        else:
            rows, lse = merge(mine(index), arrived(way, r, step - 1))
            o_out[way, r, step] = rows.astype(BF16)
            l_out[way, r, step] = jnp.transpose(jnp.broadcast_to(lse, (ROWS, 128)))[:8]
            o_src, l_src = o_out.at[way, r, step], l_out.at[way, r, step]
        device = dev_zu if way == 0 else dev_zd
        copies[way, r, step] = (
            send(
                o_src,
                o_in.at[way, r, step],
                o_send.at[way, r, step],
                o_recv.at[way, r, step],
                device,
            ),
            send(
                l_src,
                l_in.at[way, r, step],
                l_send.at[way, r, step],
                l_recv.at[way, r, step],
                device,
            ),
        )

    for step in range(4):
        for way, r in ((0, 0), (1, 1), (1, 0), (0, 1)):
            if step < reach[way, r]:
                hop(way, r, step)

    take_wout.wait()
    for r in range(2):
        value = mine(2 * z + r)
        value = merge(value, arrived(0, r, reach[0, r] - 1))
        value = merge(value, arrived(1, r, reach[1, r] - 1))
        rows = value[0].astype(BF16)
        total = jnp.dot(rows[:NEW], wout[:HEAD], preferred_element_type=F32)
        total = total + jnp.dot(rows[NEW:], wout[HEAD:], preferred_element_type=F32)
        total = total.astype(BF16)
        p_out[2 * r] = total[:OWN]
        p_out[2 * r + 1] = total[OWN:]

    p_copies = [
        send(
            p_out.at[x_peers[step][1]],
            p_in.at[step],
            p_send.at[step],
            p_recv.at[step],
            x_peers[step],
        )
        for step in range(NX - 1)
    ]
    take_wgate.wait()
    take_wproj.wait()
    projected = p_out[x].astype(F32)
    for step in range(NX - 1):
        p_copies[step].wait_recv()
        projected = projected + p_in[step].astype(F32)
    combined = (base_ref[...] + norm_rows(projected) * post_gain_ref[...]) * math.sqrt(0.5)
    gate_in = jnp.dot(combined.astype(BF16), wgate[...], preferred_element_type=F32)
    own_rows = pl.ds(pl.multiple_of(x * OWN, OWN), OWN)
    gated = jax.nn.gelu(gate_in, approximate=True) * ple_ref[own_rows, :].astype(F32)
    ple_out = jnp.dot(gated.astype(BF16), wproj[...], preferred_element_type=F32)
    result = (combined + norm_rows(ple_out) * ple_gain_ref[...]).astype(BF16)
    for k in range(NX):
        res[k] = result[:, k * SHARE : (k + 1) * SHARE]
    r_copies = [
        send(
            res.at[x_peers[step][1]],
            out_ref.at[own_rows],
            r_send.at[step],
            r_recv.at[step],
            x_peers[step],
        )
        for step in range(NX - 1)
    ]
    out_ref[own_rows, :] = res[x]
    for copy in r_copies:
        copy.wait_recv()
    for copy in p_copies + r_copies:
        copy.wait_send()
    for o_copy, l_copy in copies.values():
        o_copy.wait_send()
        l_copy.wait_send()


def any_spec():
    return pl.BlockSpec(memory_space=pl.ANY)


def vmem_spec():
    return pl.BlockSpec(memory_space=pltpu.VMEM)


def smem_spec():
    return pl.BlockSpec(memory_space=pltpu.SMEM)


def shards(
    hidden_in,
    ple_in,
    group_map,
    prompt_len,
    cache,
    w_query,
    key_value_weight,
    w_out,
    in_gain,
    q_gain,
    k_gain,
    post_gain,
    laurel_left,
    laurel_right,
    laurel_gain,
    w_plgate,
    w_plproj,
    ple_gain,
):
    inverse = np.power(THETA, -np.arange(HALF) / HALF).astype(np.float32)[None, :]
    dma = pltpu.SemaphoreType.DMA
    kv, queries, fresh, base, meta = pl.pallas_call(
        gather_kernel,
        name="gather_kernel",
        out_shape=(
            jax.ShapeDtypeStruct((2, NY, NC, GROUPS, BLOCK, HEAD), BF16),
            jax.ShapeDtypeStruct((NZ, 2, 2, NEW, HEAD), BF16),
            jax.ShapeDtypeStruct((2, ROWS, HEAD), BF16),
            jax.ShapeDtypeStruct((OWN, WIDTH), F32),
            jax.ShapeDtypeStruct((2, 2 * NZ), jnp.int32),
        ),
        in_specs=[smem_spec()] * 2 + [vmem_spec()] * 7 + [any_spec()] * 4,
        out_specs=(any_spec(), any_spec(), any_spec(), vmem_spec(), smem_spec()),
        scratch_shapes=[
            pltpu.VMEM((NX, ROWS, SHARE), BF16),
            pltpu.VMEM((NX, ROWS, SHARE), BF16),
            pltpu.VMEM((WIDTH, 2 * HEAD), BF16),
            pltpu.VMEM((WIDTH, HEAD), BF16),
            pltpu.VMEM((GROUPS, BLOCK, HEAD), BF16),
            pltpu.VMEM((2, 2, NEW, HEAD), BF16),
            pltpu.VMEM((ROWS, HEAD), BF16),
            dma((4,)),
            dma((3,)),
            dma((3,)),
            dma((8,)),
            dma((8,)),
            dma((8,)),
            dma((8,)),
            dma((2, 4, 2)),
            dma((2, 4, 2)),
            dma,
            dma,
        ],
        compiler_params=pltpu.CompilerParams(collective_id=0, has_side_effects=True),
    )(
        group_map,
        prompt_len,
        jnp.asarray(inverse),
        in_gain[None, :],
        q_gain[None, :],
        k_gain[None, :],
        laurel_left,
        laurel_right,
        laurel_gain[None, :],
        hidden_in,
        cache,
        w_query,
        key_value_weight,
    )
    requests = 2 * NZ
    part, lse = pl.pallas_call(
        attend_kernel,
        name="attend_kernel",
        out_shape=(
            jax.ShapeDtypeStruct((requests, ROWS, HEAD), BF16),
            jax.ShapeDtypeStruct((requests, 8, ROWS), F32),
        ),
        grid_spec=pltpu.PrefetchScalarGridSpec(
            num_scalar_prefetch=1,
            grid=(requests,),
            in_specs=[
                pl.BlockSpec(
                    (1, 1, 2, NEW, HEAD), lambda i, m: (lax.div(i, 2), lax.rem(i, 2), 0, 0, 0)
                ),
                pl.BlockSpec((1, NY, NC, 1, BLOCK, HEAD), lambda i, m: (0, 0, 0, m[0, i], 0, 0)),
                pl.BlockSpec((1, NY, NC, 1, BLOCK, HEAD), lambda i, m: (1, 0, 0, m[0, i], 0, 0)),
                pl.BlockSpec((2, ROWS, HEAD), lambda i, m: (0, 0, 0)),
            ],
            out_specs=[
                pl.BlockSpec((1, ROWS, HEAD), lambda i, m: (i, 0, 0)),
                pl.BlockSpec((1, 8, ROWS), lambda i, m: (i, 0, 0)),
            ],
            scratch_shapes=[
                pltpu.VMEM((ROWS, 128), F32),
                pltpu.VMEM((ROWS, 128), F32),
                pltpu.VMEM((ROWS, HEAD), F32),
            ],
        ),
        compiler_params=pltpu.CompilerParams(dimension_semantics=("arbitrary",)),
    )(meta, queries, kv, kv, fresh)
    hops = (2, 2, 4)
    return pl.pallas_call(
        finish_kernel,
        name="finish_kernel",
        out_shape=jax.ShapeDtypeStruct((ROWS, SHARE), BF16),
        in_specs=[any_spec()] + [vmem_spec()] * 5 + [any_spec()] * 3,
        out_specs=vmem_spec(),
        scratch_shapes=[
            pltpu.VMEM((requests, ROWS, HEAD), BF16),
            pltpu.VMEM((2 * HEAD, WIDTH), BF16),
            pltpu.VMEM((WIDTH, HEAD), BF16),
            pltpu.VMEM((HEAD, WIDTH), BF16),
            pltpu.VMEM(hops + (ROWS, HEAD), BF16),
            pltpu.VMEM(hops + (8, ROWS), F32),
            pltpu.VMEM(hops + (ROWS, HEAD), BF16),
            pltpu.VMEM(hops + (8, ROWS), F32),
            pltpu.VMEM((NX, OWN, WIDTH), BF16),
            pltpu.VMEM((NX - 1, OWN, WIDTH), BF16),
            pltpu.VMEM((NX, OWN, SHARE), BF16),
            dma((4,)),
            dma(hops),
            dma(hops),
            dma(hops),
            dma(hops),
            dma((3,)),
            dma((3,)),
            dma((3,)),
            dma((3,)),
        ],
        compiler_params=pltpu.CompilerParams(collective_id=1, has_side_effects=True),
    )(
        part,
        lse,
        base,
        ple_in,
        post_gain[None, :],
        ple_gain[None, :],
        w_out,
        w_plgate,
        w_plproj,
    )


def solution(mesh):
    placed = (
        P("seq", "head"),
        P("seq", None),
        P(),
        P(),
        P(None, "seq", "head"),
        P(None, "head"),
        P(None, "head"),
        P("head", None),
        P(),
        P(),
        P(),
        P(),
        P(),
        P(),
        P(),
        P(),
        P(),
        P(),
    )
    return jax.shard_map(
        shards, mesh=mesh, in_specs=placed, out_specs=P("seq", "head"), check_vma=False
    )
```
